32 devices in a mesh: row: 4 (over x, core), col: 8 (over z, y).
Axes of the slice: x: 2, y: 2, z: 4, core: 2. Of those that a mesh axis runs over, the one named last changes fastest.
Arguments:
- solution: float32 [16384, 128], P(('row', 'col')), may hold values from -6 to 6
- right_side: float32 [16384, 128], P(('row', 'col')), may hold values from -6 to 6
- block_values: bfloat16 [128, 32, 128, 128], P('row', 'col'), may hold values from -0.09375 to 0.09375
- block_columns: int32 [128, 32], P('row', 'col'), may hold values from 0 to 127, as said below
- row_order: int32 [16384], P(('row', 'col')), may hold values from 0 to 16383, as said below
- tri_inverses: bfloat16 [8192, 12288], P(('row', 'col')), may hold values from -1 to 2
- lower_updates: bfloat16 [4096, 8192], P(None, ('row', 'col')), may hold values from -0.09375 to 0.09375
- upper_updates: bfloat16 [8192, 4096], P(('row', 'col')), may hold values from -0.09375 to 0.09375
- update_rows: int32 [1, 8192], replicated, may hold values from 0 to 8191, as said below
Outputs:
- refined: float32 [16384, 128], P(('row', 'col'))
- residual: float32 [16384, 128], P(('row', 'col'))
The draws below stay inside these ranges and needn't reach their ends.
Inputs may be any that keep to these rules, and one draw needn't show every extreme that they name: `block_columns`: for block row i and slot s, the named block b satisfies (b // 4) % (8) == s // 4. `row_order`: each aligned block of 512 entries is a permutation of that block's own positions. `update_rows`: in row k, each aligned block of 2^k * 4096 entries holds distinct values below 2^(k+1) * 4096.
All inputs are finite; a program needn't handle non-finite values.
Results may differ from the reference program's by a relative error of at most 0.02.
Values may be sent and summed in bfloat16 or wider, within the bound.
No kernel may reach another device: no remote copies, remote signals or barrier semaphores. Data moves between devices by JAX's collectives and lax.ppermute only.
A program may use at most 128 MiB of HBM per device.

```python
import math
import jax
import jax.numpy as jnp
from jax import lax

S = 4096
NRHS = 128
BLOCK = 128
KBC = 4
LEVELS = 2
SR = 256
ROWS_DEV = 512
NU = 16384
LEVEL_ROWS = 8192
NBR = 128
KB = 32
BPD = 4
UPD_ROWS = 4096
TRI_COLS = 12288
N_ROW = 4


def draw_block_columns(key, part):
    col_groups = KB // KBC
    row_groups = NU // (col_groups * ROWS_DEV)
    key_owner, key_within = jax.random.split(key)
    owner_row = jax.random.randint(key_owner, (NBR, KB), 0, row_groups)
    within = jax.random.randint(key_within, (NBR, KB), 0, BPD)
    col_group = lax.broadcasted_iota(jnp.int32, (NBR, KB), 1) // KBC
    return ((owner_row * col_groups + col_group) * BPD + within).astype(jnp.int32)


def draw_row_order(key, part):
    block_count = NU // ROWS_DEV
    subkeys = jax.random.split(jax.random.fold_in(key, 11), block_count)
    shuffled = jax.vmap(lambda single: jax.random.permutation(single, ROWS_DEV))(subkeys)
    offsets = (jnp.arange(block_count, dtype=jnp.int32) * ROWS_DEV)[:, None]
    return (shuffled.astype(jnp.int32) + offsets).reshape(NU)


def draw_update_rows(key, part):
    layers = []
    for depth_k in range(LEVELS - 1):
        span_rows = S * 2 ** depth_k
        fronts = LEVEL_ROWS // span_rows
        subkeys = jax.random.split(jax.random.fold_in(key, 100 + depth_k), 2 * fronts)

        def choose(key_first, key_second):
            picked = jax.random.permutation(key_first, 2 * span_rows - 1)[:span_rows - 1]
            chosen = jnp.concatenate([picked, jnp.full((1,), 2 * span_rows - 1, picked.dtype)])
            return jax.random.permutation(key_second, chosen)
        level_rows = jax.vmap(choose)(subkeys[:fronts], subkeys[fronts:])
        layers.append(level_rows.reshape(LEVEL_ROWS).astype(jnp.int32))
    return jnp.stack(layers, 0)


def draw_tri_inverses(key, part):
    key_base = jax.random.fold_in(jax.random.fold_in(key, 7), 0)
    key_diag = jax.random.fold_in(jax.random.fold_in(key, 7), 2)
    base = jnp.clip(jax.random.normal(key_base, (LEVEL_ROWS, TRI_COLS), jnp.float32), -6.0, 6.0)
    pieces = []
    for depth_k in range(LEVELS):
        span_rows = S * 2 ** depth_k
        offset_col = S * (2 ** depth_k - 1)
        segment = base[:, offset_col:offset_col + span_rows] / math.sqrt(span_rows)
        row_ids = lax.broadcasted_iota(jnp.int32, (LEVEL_ROWS, 1), 0) % span_rows
        col_ids = lax.broadcasted_iota(jnp.int32, (1, span_rows), 1)
        diagonal = jax.random.uniform(jax.random.fold_in(key_diag, depth_k), (LEVEL_ROWS, 1), jnp.float32, 1.0, 2.0)
        pieces.append(jnp.where(row_ids == col_ids, diagonal, segment))
    return jnp.concatenate(pieces, 1).astype(jnp.bfloat16)


def shard_levels(stream_key, dims, cuts, smallest, top_value):
    def one(dim, shards_of):
        heights = jax.random.uniform(jax.random.fold_in(jax.random.fold_in(stream_key, 6), dim), (shards_of,), jnp.float32, smallest / len(cuts), top_value / len(cuts))
        return jnp.repeat(jnp.exp(heights), dims[dim] // shards_of).reshape((-1,) + (1,) * (len(dims) - dim - 1))

    factor_of = one(*cuts[0])
    for cut in cuts[1:]:
        factor_of = factor_of * one(*cut)
    return factor_of


def bell_draw(key, dims, deviation, limit, cuts=(), held_as=jnp.bfloat16):
    gain = shard_levels(key, dims, cuts, -0.22, 0.18) if cuts else 1.0
    result = jax.random.normal(key, dims, jnp.float32) * deviation * gain
    return jnp.minimum(jnp.maximum(result, -limit), limit).astype(held_as)


def setup_inputs(seed: int = 0) -> dict:
    seeds = jax.random.split(jax.random.key(seed), 10)
    solution = bell_draw(seeds[0], (NU, NRHS), 1.0, 6.0, ((0, 32),), jnp.float32)
    right_side = bell_draw(seeds[1], (NU, NRHS), 1.0, 6.0, ((0, 32),), jnp.float32)
    block_values = bell_draw(seeds[2], (NBR, KB, BLOCK, BLOCK), (KB * BLOCK) ** -0.5, 0.09375, ((0, 4), (1, 8)))
    block_columns = draw_block_columns(jax.random.fold_in(seeds[9], 71), 0)
    row_order = draw_row_order(jax.random.fold_in(seeds[9], 71), 0)
    tri_inverses = draw_tri_inverses(jax.random.fold_in(seeds[9], 71), 0)
    lower_updates = bell_draw(seeds[6], (UPD_ROWS, LEVEL_ROWS), (S * N_ROW // 4) ** -0.5, 0.09375, ((1, 32),))
    upper_updates = bell_draw(seeds[7], (LEVEL_ROWS, UPD_ROWS), (S * N_ROW // 4) ** -0.5, 0.09375, ((0, 32),))
    update_rows = draw_update_rows(jax.random.fold_in(seeds[9], 71), 0)
    return dict(solution=solution, right_side=right_side, block_values=block_values, block_columns=block_columns, row_order=row_order, tri_inverses=tri_inverses, lower_updates=lower_updates, upper_updates=upper_updates, update_rows=update_rows)


def triangle_apply(tri_panel, vector, first_row, strict_lower):
    row_ids = first_row + lax.broadcasted_iota(jnp.int32, tri_panel.shape, 0)
    col_ids = lax.broadcasted_iota(jnp.int32, tri_panel.shape, 1)
    keep_mask = col_ids < row_ids if strict_lower else col_ids >= row_ids
    masked = jnp.where(keep_mask, tri_panel, jnp.zeros_like(tri_panel))
    return jnp.dot(masked, vector, preferred_element_type=jnp.float32)


def front_solve(tri_inverses, level_vector, depth_k, strict_lower):
    span_rows = S * 2 ** depth_k
    offset_col = S * (2 ** depth_k - 1)
    outputs = []
    for begin_row in range(0, LEVEL_ROWS, S):
        front_begin = (begin_row // span_rows) * span_rows
        tri_panel = tri_inverses[begin_row:begin_row + S, offset_col:offset_col + span_rows]
        vector = level_vector[front_begin:front_begin + span_rows]
        outputs.append(triangle_apply(tri_panel, vector, begin_row - front_begin, strict_lower))
    return jnp.concatenate(outputs, 0)


def parent_positions(update_rows, depth_k):
    span_rows = S * 2 ** depth_k
    places = jnp.arange(LEVEL_ROWS, dtype=jnp.int32)
    return ((places // (2 * span_rows)) * (2 * span_rows)).astype(jnp.int32) + update_rows[depth_k].astype(jnp.int32)


def reference(solution, right_side, block_values, block_columns, row_order, tri_inverses, lower_updates, upper_updates, update_rows):
    solution_blocks = solution.reshape(NBR, BLOCK, NRHS)
    applied = jnp.zeros((NBR, BLOCK, NRHS), jnp.float32)
    for slot_idx in range(KB):
        picked = solution_blocks[block_columns[:, slot_idx]]
        values = block_values[:, slot_idx].astype(jnp.float32)
        applied = applied + jnp.einsum("ikl,iln->ikn", values, picked, precision=lax.Precision.HIGHEST)
    residual = right_side - applied.reshape(NU, NRHS)
    permuted = residual[row_order]
    stacked = permuted.reshape(NU // ROWS_DEV, LEVELS, SR, NRHS)
    lowered = []
    incoming = jnp.zeros((LEVEL_ROWS, NRHS), jnp.float32)
    for depth_k in range(LEVELS):
        current = stacked[:, depth_k].reshape(LEVEL_ROWS, NRHS) - incoming
        rounded = current.astype(jnp.bfloat16)
        solved = front_solve(tri_inverses, rounded, depth_k, True) + rounded.astype(jnp.float32)
        level_lower = solved.astype(jnp.bfloat16)
        lowered.append(level_lower)
        if depth_k + 1 < LEVELS:
            span_rows = S * 2 ** depth_k
            offset_col = S * (2 ** depth_k - 1)
            partials = []
            for front_begin in range(0, LEVEL_ROWS, span_rows):
                matrix = lower_updates[offset_col:offset_col + span_rows, front_begin:front_begin + span_rows]
                partials.append(jnp.dot(matrix, level_lower[front_begin:front_begin + span_rows], preferred_element_type=jnp.float32))
            incoming = jnp.zeros((LEVEL_ROWS, NRHS), jnp.float32).at[parent_positions(update_rows, depth_k)].add(jnp.concatenate(partials, 0))
    corrections = [None] * LEVELS
    parent_values = None
    for depth_k in reversed(range(LEVELS)):
        reduced = lowered[depth_k].astype(jnp.float32)
        if depth_k + 1 < LEVELS:
            span_rows = S * 2 ** depth_k
            offset_col = S * (2 ** depth_k - 1)
            picked_rows = parent_values[parent_positions(update_rows, depth_k)]
            update_terms = []
            for front_begin in range(0, LEVEL_ROWS, span_rows):
                matrix = upper_updates[front_begin:front_begin + span_rows, offset_col:offset_col + span_rows]
                update_terms.append(jnp.dot(matrix, picked_rows[front_begin:front_begin + span_rows], preferred_element_type=jnp.float32))
            reduced = reduced - jnp.concatenate(update_terms, 0)
        rounded = reduced.astype(jnp.bfloat16)
        corrections[depth_k] = front_solve(tri_inverses, rounded, depth_k, False)
        parent_values = corrections[depth_k].astype(jnp.bfloat16)
    correction = jnp.stack([level_piece.reshape(NU // ROWS_DEV, SR, NRHS) for level_piece in corrections], 1).reshape(NU, NRHS)
    return solution + correction, residual
```

```python
import itertools

import jax
import jax.numpy as jnp
from jax import lax
from jax.sharding import PartitionSpec as P

BOTH = ("row", "col")


def flip_bit(values, bit):
    count = lax.axis_size("row") * lax.axis_size("col")
    return lax.ppermute(values, BOTH, [(i, i ^ (1 << bit)) for i in range(count)])


def groups_of(bits):
    count = lax.axis_size("row") * lax.axis_size("col")
    mask = sum(1 << b for b in bits)
    groups = []
    for base in range(count):
        if base & mask:
            continue
        group = []
        for choice in itertools.product((0, 1), repeat=len(bits)):
            group.append(base | sum(c << b for c, b in zip(choice, bits)))
        groups.append(group)
    return groups


def exchange(values, bits):
    return lax.all_to_all(values, BOTH, 0, 0, axis_index_groups=groups_of(bits))


def ordered(own, other, bit_value):
    raised = bit_value == 1
    return jnp.stack([jnp.where(raised, other, own), jnp.where(raised, own, other)])


def half(values, wanted):
    return jnp.where(wanted == 1, values[1], values[0])


def front_gather(values, bit_count):
    col_bits = lax.axis_size("col").bit_length() - 1
    row = lax.axis_index("row")
    col = lax.axis_index("col")
    seg_rows, width = values.shape
    upper = [col_bits + b for b in reversed(range(1, bit_count))]
    near = list(reversed(range(col_bits)))
    if upper:
        far = near[0]
        near = near[1:]
        values = ordered(values, flip_bit(values, far), col >> far & 1)
        far_count = 2
    else:
        values = values[None]
        far_count = 1
    count = 2 ** (len(upper) + len(near))
    spread = jnp.broadcast_to(values[None], (count,) + values.shape)
    arrived = exchange(spread, upper + near)
    both = ordered(arrived, flip_bit(arrived, col_bits), row & 1)
    both = both.reshape(2, 2 ** len(upper), 2 ** len(near), far_count, seg_rows, width)
    return both.transpose(1, 0, 3, 2, 4, 5).reshape(-1, width)


def front_reduce(placed, bit_count):
    col_bits = lax.axis_size("col").bit_length() - 1
    row = lax.axis_index("row")
    col = lax.axis_index("col")
    width = placed.shape[1]
    upper = [col_bits + b for b in reversed(range(1, bit_count))]
    far = col_bits - 1
    near = list(reversed(range(far)))
    parts = placed.reshape(2 ** len(upper), 2, 2, 2 ** len(near), -1, width)
    parts = parts.transpose(1, 0, 3, 2, 4, 5)
    core = row & 1
    other = flip_bit(half(parts, 1 - core).astype(jnp.bfloat16), col_bits)
    kept = half(parts, core) + other.astype(jnp.float32)
    kept = kept.reshape((-1,) + kept.shape[2:])
    arrived = exchange(kept.astype(jnp.bfloat16), upper + near)
    return far_sum(arrived, far)


def far_sum(arrived, far):
    side = lax.axis_index("col") >> far & 1
    summed = jnp.sum(arrived.astype(jnp.float32), axis=0)
    other = flip_bit(half(summed, 1 - side).astype(jnp.bfloat16), far)
    return half(summed, side) + other.astype(jnp.float32)


def column_reduce(values):
    col_bits = lax.axis_size("col").bit_length() - 1
    far = col_bits - 1
    near = list(reversed(range(far)))
    width = values.shape[1]
    parts = values.astype(jnp.bfloat16).reshape(2, 2 ** len(near), -1, width).transpose(1, 0, 2, 3)
    return far_sum(exchange(parts, near), far)


def row_gather(values):
    col_bits = lax.axis_size("col").bit_length() - 1
    row_bits = lax.axis_size("row").bit_length() - 1
    pieces = values[None]
    for b in reversed(range(row_bits)):
        pieces = jnp.stack([pieces, flip_bit(pieces, col_bits + b)], 1)
        pieces = pieces.reshape((-1,) + values.shape)
    return pieces


def triangle_rows(tri_panel, full_vector, first_row, strict_lower):
    row_ids = first_row + lax.broadcasted_iota(jnp.int32, tri_panel.shape, 0)
    col_ids = lax.broadcasted_iota(jnp.int32, tri_panel.shape, 1)
    keep_mask = col_ids < row_ids if strict_lower else col_ids >= row_ids
    masked = jnp.where(keep_mask, tri_panel, jnp.zeros_like(tri_panel))
    return jnp.dot(masked, full_vector, preferred_element_type=jnp.float32)


def on_device(
    solution,
    right_side,
    block_values,
    block_columns,
    row_order,
    tri_inverses,
    lower_updates,
    upper_updates,
    update_rows,
):
    row_count = lax.axis_size("row")
    col_count = lax.axis_size("col")
    levels_count = row_count.bit_length() - 1
    per_device = solution.shape[0]
    seg_rows = per_device // levels_count
    block_size = block_values.shape[2]
    per_block = per_device // block_size
    row_index = lax.axis_index("row")
    col_index = lax.axis_index("col")
    gathered = row_gather(solution.astype(jnp.bfloat16))
    owner = block_columns // (per_block * col_count) ^ row_index
    local_block = owner * per_block + block_columns % per_block
    solution_blocks = gathered.reshape(row_count * per_block, block_size, -1)
    picked = solution_blocks[local_block]
    applied = jnp.einsum(
        "iskl,isln->ikn", block_values, picked, preferred_element_type=jnp.float32
    )
    product = column_reduce(applied.reshape(-1, applied.shape[-1]))
    residual = right_side - product
    device_index = row_index * col_count + col_index
    local_order = row_order - device_index * per_device
    permuted = residual[local_order]
    stacked = permuted.reshape(levels_count, seg_rows, -1)
    sep_bottom = 2 * col_count * seg_rows
    lowered = []
    targets_all = []
    first_rows = []
    incoming = None
    for depth_k in range(levels_count):
        groups = 2 ** (depth_k + 1)
        span_rows = sep_bottom * 2**depth_k
        offset_col = sep_bottom * (2**depth_k - 1)
        first_row = (row_index % groups * col_count + col_index) * seg_rows
        first_rows.append(first_row)
        current = stacked[depth_k]
        if depth_k > 0:
            current = current - incoming
        rounded = current.astype(jnp.bfloat16)
        front_full = front_gather(rounded, depth_k + 1)
        tri_panel = tri_inverses[:, offset_col : offset_col + span_rows]
        solved_rows = triangle_rows(tri_panel, front_full, first_row, True) + rounded.astype(
            jnp.float32
        )
        lower_rows = solved_rows.astype(jnp.bfloat16)
        lowered.append(lower_rows)
        if depth_k + 1 < levels_count:
            front_idx = row_index // groups
            chosen = lax.dynamic_slice_in_dim(
                update_rows[depth_k], front_idx * span_rows, span_rows
            )
            targets_all.append(chosen)
            partials = jnp.dot(
                lower_updates[offset_col : offset_col + span_rows],
                lower_rows,
                preferred_element_type=jnp.float32,
            )
            placed = jnp.zeros((2 * span_rows, partials.shape[1]), jnp.float32)
            placed = placed.at[chosen].add(partials)
            incoming = front_reduce(placed, depth_k + 2)
    corrections = [None] * levels_count
    parent_rows = None
    for depth_k in reversed(range(levels_count)):
        span_rows = sep_bottom * 2**depth_k
        offset_col = sep_bottom * (2**depth_k - 1)
        rounded = lowered[depth_k]
        if depth_k + 1 < levels_count:
            parent_full = front_gather(parent_rows, depth_k + 2)
            picked_rows = parent_full[targets_all[depth_k]]
            reduced = rounded.astype(jnp.float32) - jnp.dot(
                upper_updates[:, offset_col : offset_col + span_rows],
                picked_rows,
                preferred_element_type=jnp.float32,
            )
            rounded = reduced.astype(jnp.bfloat16)
        full_vector = front_gather(rounded, depth_k + 1)
        tri_panel = tri_inverses[:, offset_col : offset_col + span_rows]
        upper_rows = triangle_rows(tri_panel, full_vector, first_rows[depth_k], False)
        corrections[depth_k] = upper_rows
        parent_rows = upper_rows.astype(jnp.bfloat16)
    correction = jnp.concatenate(corrections, 0)
    return (solution + correction, residual)


def solution(mesh):
    in_specs = (
        P(BOTH, None),
        P(BOTH, None),
        P("row", "col", None, None),
        P("row", "col"),
        P(BOTH),
        P(BOTH, None),
        P(None, BOTH),
        P(BOTH, None),
        P(),
    )
    out_specs = (P(BOTH, None), P(BOTH, None))
    return jax.shard_map(
        on_device, mesh=mesh, in_specs=in_specs, out_specs=out_specs, check_vma=False
    )
```

```python
import functools
import itertools

import jax
import jax.numpy as jnp
from jax import lax
from jax.experimental import pallas as pl
from jax.experimental.pallas import tpu as pltpu
from jax.sharding import PartitionSpec as P

BOTH = ("row", "col")


def flip_bit(values, bit):
    count = lax.axis_size("row") * lax.axis_size("col")
    return lax.ppermute(values, BOTH, [(i, i ^ (1 << bit)) for i in range(count)])


def groups_of(bits):
    count = lax.axis_size("row") * lax.axis_size("col")
    mask = sum(1 << b for b in bits)
    groups = []
    for base in range(count):
        if base & mask:
            continue
        group = []
        for choice in itertools.product((0, 1), repeat=len(bits)):
            group.append(base | sum(c << b for c, b in zip(choice, bits)))
        groups.append(group)
    return groups


def exchange(values, bits):
    return lax.all_to_all(values, BOTH, 0, 0, axis_index_groups=groups_of(bits))


def ordered(own, other, bit_value):
    raised = bit_value == 1
    return jnp.stack([jnp.where(raised, other, own), jnp.where(raised, own, other)])


def col_bit_count():
    return lax.axis_size("col").bit_length() - 1


def near_bits():
    return list(reversed(range(col_bit_count() - 1)))


def upper_bits(bit_count):
    return [col_bit_count() + b for b in reversed(range(1, bit_count))]


def far_side():
    return lax.axis_index("col") >> (col_bit_count() - 1)


def gather_halves(values, bit_count):
    col_bits = col_bit_count()
    other = flip_bit(values, col_bits - 1)
    values = jnp.stack([values, other])
    bits = upper_bits(bit_count) + near_bits()
    spread = jnp.broadcast_to(values[None], (2 ** len(bits),) + values.shape)
    arrived = exchange(spread, bits)
    return arrived, flip_bit(arrived, col_bits)


def arrival_rows(rows, bit_count, seg_rows):
    near_count = 2 ** len(near_bits())
    within = rows % seg_rows
    near = rows // seg_rows % near_count
    far = rows // (seg_rows * near_count) % 2 ^ far_side()
    core = rows // (seg_rows * near_count * 2) % 2 ^ lax.axis_index("row") & 1
    upper = rows // (seg_rows * near_count * 4)
    upper_count = 2 ** (bit_count - 1)
    return (((core * upper_count + upper) * near_count + near) * 2 + far) * seg_rows + within


def front_gather(values, bit_count):
    col_bits = col_bit_count()
    row = lax.axis_index("row")
    seg_rows, width = values.shape
    if bit_count > 1:
        arrived, other = gather_halves(values, bit_count)
        side = far_side()
        pieces = ordered(arrived, other, row & 1)
        pieces = ordered(pieces[:, :, 0], pieces[:, :, 1], side)
        pieces = pieces.reshape(2, 2, 2 ** (bit_count - 1), -1, seg_rows, width)
        return pieces.transpose(2, 1, 0, 3, 4, 5).reshape(-1, width)
    bits = list(reversed(range(col_bits)))
    spread = jnp.broadcast_to(values[None], (2**col_bits,) + values.shape)
    arrived = exchange(spread, bits)
    return ordered(arrived, flip_bit(arrived, col_bits), row & 1).reshape(-1, width)


def far_sum(arrived):
    summed = jnp.sum(arrived.astype(jnp.float32), axis=0)
    other = flip_bit(summed[1].astype(jnp.bfloat16), col_bit_count() - 1)
    return summed[0] + other.astype(jnp.float32)


def front_reduce(kept, sent, bit_count, seg_rows):
    other = flip_bit(sent, col_bit_count())
    total = (kept.astype(jnp.float32) + other.astype(jnp.float32)).astype(jnp.bfloat16)
    bits = upper_bits(bit_count) + near_bits()
    total = total.reshape(2 ** len(bits), 2, seg_rows, -1)
    return far_sum(exchange(total, bits))


def row_gather(values):
    col_bits = col_bit_count()
    row_bits = lax.axis_size("row").bit_length() - 1
    pieces = values[None]
    for b in reversed(range(row_bits)):
        pieces = jnp.stack([pieces, flip_bit(pieces, col_bits + b)], 1)
        pieces = pieces.reshape((-1,) + values.shape)
    return pieces


def product_kernel(near_count, picks_ref, side_ref, values_ref, blocks_ref, out_ref):
    step = pl.program_id(0)
    rows, slots, size, _ = values_ref.shape
    for r in range(rows):
        left = [values_ref[r, s] for s in range(slots)]
        right = [blocks_ref[picks_ref[(step * rows + r) * slots + s]] for s in range(slots)]
        total = jnp.dot(
            jnp.concatenate(left, 1),
            jnp.concatenate(right, 0),
            preferred_element_type=jnp.float32,
        )
        out_ref[pl.ds(r * size, size), :] = total.astype(jnp.bfloat16)


def block_product(values, blocks, picks, per_block):
    block_rows, slots, size, _ = values.shape
    width = blocks.shape[2]
    near_count = 2 ** len(near_bits())
    steps = block_rows // per_block

    def place(i, picks_ref, side_ref):
        return (i % near_count * 2 + (i // near_count ^ side_ref[0]), 0)

    return pl.pallas_call(
        functools.partial(product_kernel, near_count),
        out_shape=jax.ShapeDtypeStruct((block_rows * size, width), jnp.bfloat16),
        grid_spec=pltpu.PrefetchScalarGridSpec(
            num_scalar_prefetch=2,
            grid=(steps,),
            in_specs=[
                pl.BlockSpec((per_block, slots, size, size), lambda i, *_: (i, 0, 0, 0)),
                pl.BlockSpec(blocks.shape, lambda i, *_: (0, 0, 0)),
            ],
            out_specs=pl.BlockSpec((per_block * size, width), place),
        ),
    )(picks.reshape(-1), far_side().reshape(1), values, blocks)


UNROLL = 16


def scatter_kernel(places_ref, lower_ref, rows_ref, kept_ref, sent_ref, part, total):
    step = pl.program_id(0)
    chunk = part.shape[0]

    @pl.when(step == 0)
    def _():
        total[...] = jnp.zeros_like(total)

    part[...] = jnp.dot(lower_ref[...], rows_ref[...], preferred_element_type=jnp.float32)

    def move(i, carry):
        for j in range(UNROLL):
            u = i * UNROLL + j
            total[pl.ds(places_ref[step * chunk + u], 1), :] = part[pl.ds(u, 1), :]
        return carry

    lax.fori_loop(0, chunk // UNROLL, move, 0)

    @pl.when(step == pl.num_programs(0) - 1)
    def _():
        count = kept_ref.shape[0]
        kept_ref[...] = total[:count].astype(jnp.bfloat16)
        sent_ref[...] = total[count:].astype(jnp.bfloat16)


def scatter_update(lower, rows, places):
    span, seg_rows = lower.shape
    width = rows.shape[1]
    chunk = min(span, 512)
    return pl.pallas_call(
        scatter_kernel,
        out_shape=[jax.ShapeDtypeStruct((span, width), jnp.bfloat16)] * 2,
        grid_spec=pltpu.PrefetchScalarGridSpec(
            num_scalar_prefetch=1,
            grid=(span // chunk,),
            in_specs=[
                pl.BlockSpec((chunk, seg_rows), lambda i, *_: (i, 0)),
                pl.BlockSpec((seg_rows, width), lambda i, *_: (0, 0)),
            ],
            out_specs=[pl.BlockSpec((span, width), lambda i, *_: (0, 0))] * 2,
            scratch_shapes=[
                pltpu.VMEM((chunk, width), jnp.float32),
                pltpu.VMEM((2 * span, width), jnp.float32),
            ],
        ),
    )(places, lower, rows)


def pick_kernel(places_ref, upper_ref, own_ref, other_ref, base_ref, out_ref, full, part, total):
    step = pl.program_id(0)
    chunk = part.shape[0]

    @pl.when(step == 0)
    def _():
        count = own_ref.shape[0]
        full[:count] = own_ref[...].astype(jnp.float32)
        full[count:] = other_ref[...].astype(jnp.float32)
        total[...] = base_ref[...].astype(jnp.float32)

    def move(i, carry):
        for j in range(UNROLL):
            u = i * UNROLL + j
            part[pl.ds(u, 1), :] = full[pl.ds(places_ref[step * chunk + u], 1), :]
        return carry

    lax.fori_loop(0, chunk // UNROLL, move, 0)
    total[...] -= jnp.dot(
        upper_ref[...], part[...].astype(jnp.bfloat16), preferred_element_type=jnp.float32
    )

    @pl.when(step == pl.num_programs(0) - 1)
    def _():
        out_ref[...] = total[...].astype(jnp.bfloat16)


def pick_update(upper, own, other, places, base):
    seg_rows, span = upper.shape
    width = base.shape[1]
    chunk = min(span, 512)
    own = own.reshape(-1, width)
    other = other.reshape(-1, width)
    return pl.pallas_call(
        pick_kernel,
        out_shape=jax.ShapeDtypeStruct((seg_rows, width), jnp.bfloat16),
        grid_spec=pltpu.PrefetchScalarGridSpec(
            num_scalar_prefetch=1,
            grid=(span // chunk,),
            in_specs=[
                pl.BlockSpec((seg_rows, chunk), lambda i, *_: (0, i)),
                pl.BlockSpec(own.shape, lambda i, *_: (0, 0)),
                pl.BlockSpec(other.shape, lambda i, *_: (0, 0)),
                pl.BlockSpec((seg_rows, width), lambda i, *_: (0, 0)),
            ],
            out_specs=pl.BlockSpec((seg_rows, width), lambda i, *_: (0, 0)),
            scratch_shapes=[
                pltpu.VMEM((2 * span, width), jnp.float32),
                pltpu.VMEM((chunk, width), jnp.float32),
                pltpu.VMEM((seg_rows, width), jnp.float32),
            ],
        ),
    )(places, upper, own, other, base)


def triangle_rows(tri_panel, full_vector, first_row, strict_lower):
    row_ids = first_row + lax.broadcasted_iota(jnp.int32, tri_panel.shape, 0)
    col_ids = lax.broadcasted_iota(jnp.int32, tri_panel.shape, 1)
    keep_mask = col_ids < row_ids if strict_lower else col_ids >= row_ids
    masked = jnp.where(keep_mask, tri_panel, jnp.zeros_like(tri_panel))
    return jnp.dot(masked, full_vector, preferred_element_type=jnp.float32)


def on_device(
    solution,
    right_side,
    block_values,
    block_columns,
    row_order,
    tri_inverses,
    lower_updates,
    upper_updates,
    update_rows,
):
    row_count = lax.axis_size("row")
    col_count = lax.axis_size("col")
    levels_count = row_count.bit_length() - 1
    per_device = solution.shape[0]
    seg_rows = per_device // levels_count
    block_size = block_values.shape[2]
    per_block = per_device // block_size
    row_index = lax.axis_index("row")
    col_index = lax.axis_index("col")
    gathered = row_gather(solution.astype(jnp.bfloat16))
    owner = block_columns // (per_block * col_count) ^ row_index
    local_block = owner * per_block + block_columns % per_block
    solution_blocks = gathered.reshape(row_count * per_block, block_size, -1)
    applied = block_product(block_values, solution_blocks, local_block, per_block)
    applied = applied.reshape(-1, 2, per_device, applied.shape[-1])
    product = far_sum(exchange(applied, near_bits()))
    residual = right_side - product
    device_index = row_index * col_count + col_index
    local_order = row_order - device_index * per_device
    permuted = residual[local_order]
    stacked = permuted.reshape(levels_count, seg_rows, -1)
    sep_bottom = 2 * col_count * seg_rows
    lowered = []
    targets_all = []
    first_rows = []
    incoming = None
    for depth_k in range(levels_count):
        groups = 2 ** (depth_k + 1)
        span_rows = sep_bottom * 2**depth_k
        offset_col = sep_bottom * (2**depth_k - 1)
        first_row = (row_index % groups * col_count + col_index) * seg_rows
        first_rows.append(first_row)
        current = stacked[depth_k]
        if depth_k > 0:
            current = current - incoming
        rounded = current.astype(jnp.bfloat16)
        front_full = front_gather(rounded, depth_k + 1)
        tri_panel = tri_inverses[:, offset_col : offset_col + span_rows]
        solved_rows = triangle_rows(tri_panel, front_full, first_row, True) + rounded.astype(
            jnp.float32
        )
        lower_rows = solved_rows.astype(jnp.bfloat16)
        lowered.append(lower_rows)
        if depth_k + 1 < levels_count:
            front_idx = row_index // groups
            chosen = lax.dynamic_slice_in_dim(
                update_rows[depth_k], front_idx * span_rows, span_rows
            )
            places = arrival_rows(chosen, depth_k + 2, seg_rows)
            targets_all.append(places)
            kept, sent = scatter_update(
                lower_updates[offset_col : offset_col + span_rows], lower_rows, places
            )
            incoming = front_reduce(kept, sent, depth_k + 2, seg_rows)
    corrections = [None] * levels_count
    parent_rows = None
    for depth_k in reversed(range(levels_count)):
        span_rows = sep_bottom * 2**depth_k
        offset_col = sep_bottom * (2**depth_k - 1)
        rounded = lowered[depth_k]
        if depth_k + 1 < levels_count:
            own, other = gather_halves(parent_rows, depth_k + 2)
            rounded = pick_update(
                upper_updates[:, offset_col : offset_col + span_rows],
                own,
                other,
                targets_all[depth_k],
                rounded,
            )
        full_vector = front_gather(rounded, depth_k + 1)
        tri_panel = tri_inverses[:, offset_col : offset_col + span_rows]
        upper_rows = triangle_rows(tri_panel, full_vector, first_rows[depth_k], False)
        corrections[depth_k] = upper_rows
        parent_rows = upper_rows.astype(jnp.bfloat16)
    correction = jnp.concatenate(corrections, 0)
    return (solution + correction, residual)


def solution(mesh):
    in_specs = (
        P(BOTH, None),
        P(BOTH, None),
        P("row", "col", None, None),
        P("row", "col"),
        P(BOTH),
        P(BOTH, None),
        P(None, BOTH),
        P(BOTH, None),
        P(),
    )
    out_specs = (P(BOTH, None), P(BOTH, None))
    return jax.shard_map(
        on_device, mesh=mesh, in_specs=in_specs, out_specs=out_specs, check_vma=False
    )
```

```python
import functools
import itertools

import jax
import jax.numpy as jnp
from jax import lax
from jax.experimental import pallas as pl
from jax.experimental.pallas import tpu as pltpu
from jax.sharding import PartitionSpec as P

BOTH = ("row", "col")


def col_bit_count():
    return lax.axis_size("col").bit_length() - 1


def near_bits():
    return list(range(col_bit_count() - 1))


def upper_bits(bit_count):
    return [col_bit_count() + b for b in range(1, bit_count)]


def far_mask():
    return 1 << (col_bit_count() - 1)


def core_mask():
    return 1 << col_bit_count()


def masks_of(bits):
    masks = [sum(c << b for c, b in zip(choice, bits)) for choice in itertools.product((0, 1), repeat=len(bits))]
    return sorted(masks, key=lambda m: (m != 0, -bin(m).count("1"), m))


def send(values, mask):
    count = lax.axis_size("row") * lax.axis_size("col")
    return lax.ppermute(values, BOTH, [(i, i ^ mask) for i in range(count)])


def relay_bits(bit_count):
    bits = upper_bits(bit_count) + near_bits()
    if bit_count == 1:
        return bits, None, None
    return bits, min(bits), max(bits)


def gather_pieces(values, bit_count):
    bits, own_relay, far_relay = relay_bits(bit_count)
    far = send(values, far_mask())
    pieces = []
    for base, start, relay in ((values, 0, own_relay), (far, far_mask(), far_relay)):
        direct = masks_of([b for b in bits if b != relay])
        arrived = [base] + [send(base, m) for m in direct[1:]]
        masks = [start ^ m for m in direct]
        if relay is None:
            pieces += [([m], piece) for m, piece in zip(masks, arrived)]
        else:
            joined = jnp.concatenate(arrived, 0)
            step = 1 << relay
            pieces.append((masks, joined))
            pieces.append(([m ^ step for m in masks], send(joined, step)))
    core = core_mask()
    return pieces + [([m ^ core for m in masks], send(piece, core)) for masks, piece in pieces]


def added(first, *others):
    total = first.astype(jnp.float32)
    for other in others:
        total = total + other.astype(jnp.float32)
    return total


def reduce_order(bit_count):
    bits, own_relay, far_relay = relay_bits(bit_count)
    orders = []
    for start, relay in ((far_mask(), far_relay), (0, own_relay)):
        direct = masks_of([b for b in bits if b != relay])
        orders.append([start ^ m ^ step for step in (0, 1 << relay) for m in direct])
    return orders


def front_reduce(kept, sent, bit_count, seg_rows):
    bits, own_relay, far_relay = relay_bits(bit_count)
    sums = []
    for keep, give, relay in zip(kept, sent, (far_relay, own_relay)):
        total = added(keep, send(give, core_mask())).astype(jnp.bfloat16)
        middle = total.shape[0] // 2
        total = added(total[:middle], send(total[middle:], 1 << relay)).astype(jnp.bfloat16)
        parts = total.reshape(-1, seg_rows, total.shape[1])
        direct = masks_of([b for b in bits if b != relay])
        moved = [send(parts[i], m) for i, m in enumerate(direct) if m]
        sums.append(added(parts[0], *moved))
    return added(sums[1], send(sums[0].astype(jnp.bfloat16), far_mask()))


def column_reduce(parts):
    direct = masks_of(near_bits())
    sums = []
    for start in (far_mask(), 0):
        moved = [send(parts[start ^ m], m) for m in direct[1:]]
        sums.append(added(parts[start], *moved))
    return added(sums[1], send(sums[0].astype(jnp.bfloat16), far_mask()))


def row_gather(values):
    row_bits = lax.axis_size("row").bit_length() - 1
    pieces = [values]
    for b in reversed(range(row_bits)):
        pieces = [p for piece in pieces for p in (piece, send(piece, core_mask() << b))]
    return jnp.stack(pieces)


def product_kernel(picks_ref, side_ref, values_ref, blocks_ref, out_ref):
    step = pl.program_id(0)
    rows, slots, size, _ = values_ref.shape
    for r in range(rows):
        left = [values_ref[r, s] for s in range(slots)]
        right = [blocks_ref[picks_ref[(step * rows + r) * slots + s]] for s in range(slots)]
        total = jnp.dot(
            jnp.concatenate(left, 1),
            jnp.concatenate(right, 0),
            preferred_element_type=jnp.float32,
        )
        out_ref[pl.ds(r * size, size), :] = total.astype(jnp.bfloat16)


def block_product(values, blocks, picks, per_block):
    block_rows, slots, size, _ = values.shape
    width = blocks.shape[2]
    steps = block_rows // per_block

    def place(i, picks_ref, side_ref):
        return (i ^ side_ref[0], 0)

    return pl.pallas_call(
        product_kernel,
        out_shape=jax.ShapeDtypeStruct((block_rows * size, width), jnp.bfloat16),
        grid_spec=pltpu.PrefetchScalarGridSpec(
            num_scalar_prefetch=2,
            grid=(steps,),
            in_specs=[
                pl.BlockSpec((per_block, slots, size, size), lambda i, *_: (i, 0, 0, 0)),
                pl.BlockSpec(blocks.shape, lambda i, *_: (0, 0, 0)),
            ],
            out_specs=pl.BlockSpec((per_block * size, width), place),
        ),
    )(picks.reshape(-1), lax.axis_index("col").reshape(1), values, blocks)


UNROLL = 16


def scatter_kernel(orders, places_ref, lower_ref, rows_ref, *refs):
    outs, (part, total) = refs[:-2], refs[-2:]
    step = pl.program_id(0)
    chunk = part.shape[0]

    @pl.when(step == 0)
    def _():
        total[...] = jnp.zeros_like(total)

    part[...] = jnp.dot(lower_ref[...], rows_ref[...], preferred_element_type=jnp.float32)

    def move(i, carry):
        for j in range(UNROLL):
            u = i * UNROLL + j
            total[pl.ds(places_ref[step * chunk + u], 1), :] = part[pl.ds(u, 1), :]
        return carry

    lax.fori_loop(0, chunk // UNROLL, move, 0)

    @pl.when(step == pl.num_programs(0) - 1)
    def _():
        for order, out_ref in zip(orders, outs):
            size = out_ref.shape[0] // len(order)
            for i, m in enumerate(order):
                out_ref[i * size : (i + 1) * size] = total[m * size : (m + 1) * size].astype(
                    jnp.bfloat16
                )


def scatter_update(lower, rows, places, bit_count):
    span, seg_rows = lower.shape
    width = rows.shape[1]
    chunk = min(span, 512)
    orders = reduce_order(bit_count)
    orders = orders + [[m ^ core_mask() for m in order] for order in orders]
    count = span // 2
    outs = pl.pallas_call(
        functools.partial(scatter_kernel, orders),
        out_shape=[jax.ShapeDtypeStruct((count, width), jnp.bfloat16)] * 4,
        grid_spec=pltpu.PrefetchScalarGridSpec(
            num_scalar_prefetch=1,
            grid=(span // chunk,),
            in_specs=[
                pl.BlockSpec((chunk, seg_rows), lambda i, *_: (i, 0)),
                pl.BlockSpec((seg_rows, width), lambda i, *_: (0, 0)),
            ],
            out_specs=[pl.BlockSpec((count, width), lambda i, *_: (0, 0))] * 4,
            scratch_shapes=[
                pltpu.VMEM((chunk, width), jnp.float32),
                pltpu.VMEM((2 * span, width), jnp.float32),
            ],
        ),
        compiler_params=pltpu.CompilerParams(vmem_limit_bytes=grant(2 * span * width * 4 + 4 * span * width * 2)),
    )(places, lower, rows)
    return outs[:2], outs[2:]


def grant(size):
    return size + (6 << 20)


def pick_kernel(masks, places_ref, upper_ref, base_ref, *refs):
    pieces, (out_ref, full, part, total) = refs[:-4], refs[-4:]
    step = pl.program_id(0)
    chunk = part.shape[0]

    @pl.when(step == 0)
    def _():
        for group, piece_ref in zip(masks, pieces):
            size = piece_ref.shape[0] // len(group)
            for i, m in enumerate(group):
                full[m * size : (m + 1) * size] = piece_ref[i * size : (i + 1) * size].astype(
                    jnp.float32
                )
        total[...] = base_ref[...].astype(jnp.float32)

    def move(i, carry):
        for j in range(UNROLL):
            u = i * UNROLL + j
            part[pl.ds(u, 1), :] = full[pl.ds(places_ref[step * chunk + u], 1), :]
        return carry

    lax.fori_loop(0, chunk // UNROLL, move, 0)
    total[...] -= jnp.dot(
        upper_ref[...], part[...].astype(jnp.bfloat16), preferred_element_type=jnp.float32
    )

    @pl.when(step == pl.num_programs(0) - 1)
    def _():
        out_ref[...] = total[...].astype(jnp.bfloat16)


def whole_block(array):
    return pl.BlockSpec(array.shape, lambda *_: (0,) * array.ndim)


def pick_update(upper, pieces, places, base):
    seg_rows, span = upper.shape
    width = base.shape[1]
    chunk = min(span, 512)
    masks = [group for group, _ in pieces]
    arrays = [array for _, array in pieces]
    return pl.pallas_call(
        functools.partial(pick_kernel, masks),
        out_shape=jax.ShapeDtypeStruct((seg_rows, width), jnp.bfloat16),
        grid_spec=pltpu.PrefetchScalarGridSpec(
            num_scalar_prefetch=1,
            grid=(span // chunk,),
            in_specs=[pl.BlockSpec((seg_rows, chunk), lambda i, *_: (0, i)), whole_block(base)]
            + [whole_block(array) for array in arrays],
            out_specs=pl.BlockSpec((seg_rows, width), lambda i, *_: (0, 0)),
            scratch_shapes=[
                pltpu.VMEM((2 * span, width), jnp.float32),
                pltpu.VMEM((chunk, width), jnp.float32),
                pltpu.VMEM((seg_rows, width), jnp.float32),
            ],
        ),
        compiler_params=pltpu.CompilerParams(vmem_limit_bytes=grant(2 * span * width * 8)),
    )(places, upper, base, *arrays)


def triangle_sum(masks, offset, strict, own, tri_ref, pieces):
    seg_rows = tri_ref.shape[0]
    total = None
    for group, piece_ref in zip(masks, pieces):
        for i, m in enumerate(group):
            block = own ^ m
            start = pl.multiple_of(offset + block * seg_rows, 128)
            panel = tri_ref[:, pl.ds(start, seg_rows)]
            vector = piece_ref[i * seg_rows : (i + 1) * seg_rows, :]
            if m == 0:
                row_ids = lax.broadcasted_iota(jnp.int32, panel.shape, 0)
                col_ids = lax.broadcasted_iota(jnp.int32, panel.shape, 1)
                keep = col_ids < row_ids if strict else col_ids >= row_ids
                panel = jnp.where(keep, panel, jnp.zeros_like(panel))
            else:
                used = block < own if strict else block > own
                vector = jnp.where(used, vector, jnp.zeros_like(vector))
            term = jnp.dot(panel, vector, preferred_element_type=jnp.float32)
            total = term if total is None else total + term
    return total


def lower_kernel(masks, offset, own_ref, tri_ref, *refs):
    pieces, out_ref = refs[:-1], refs[-1]
    total = triangle_sum(masks, offset, True, own_ref[0], tri_ref, pieces)
    seg_rows = out_ref.shape[0]
    out_ref[...] = (total + pieces[0][:seg_rows].astype(jnp.float32)).astype(jnp.bfloat16)


def upper_kernel(masks, offset, own_ref, tri_ref, *refs):
    pieces, (exact_ref, out_ref) = refs[:-2], refs[-2:]
    total = triangle_sum(masks, offset, False, own_ref[0], tri_ref, pieces)
    exact_ref[...] = total
    out_ref[...] = total.astype(jnp.bfloat16)


def last_kernel(masks, offset, levels, own_ref, tri_ref, solution_ref, *refs):
    others, pieces, out_ref = refs[: levels - 1], refs[levels - 1 : -1], refs[-1]
    total = triangle_sum(masks, offset, False, own_ref[0], tri_ref, pieces)
    seg_rows = total.shape[0]
    out_ref[:seg_rows] = solution_ref[:seg_rows] + total
    for k, other in enumerate(others):
        rows = pl.ds((k + 1) * seg_rows, seg_rows)
        out_ref[rows, :] = solution_ref[rows, :] + other[...]


def triangle_apply(kernel, tri, own, pieces, outs, before=()):
    masks = [group for group, _ in pieces]
    arrays = list(before) + [array for _, array in pieces]
    size = sum(array.size * array.dtype.itemsize for array in arrays)
    return pl.pallas_call(
        functools.partial(kernel, masks),
        out_shape=outs,
        in_specs=[pl.BlockSpec(memory_space=pltpu.SMEM)]
        + [pl.BlockSpec(memory_space=pltpu.VMEM)] * (1 + len(arrays)),
        out_specs=jax.tree.map(lambda _: pl.BlockSpec(memory_space=pltpu.VMEM), outs),
        compiler_params=pltpu.CompilerParams(vmem_limit_bytes=grant(tri.size * 2 + size)),
    )(own.reshape(1), tri, *arrays)


def on_device(
    solution,
    right_side,
    block_values,
    block_columns,
    row_order,
    tri_inverses,
    lower_updates,
    upper_updates,
    update_rows,
):
    row_count = lax.axis_size("row")
    col_count = lax.axis_size("col")
    levels_count = row_count.bit_length() - 1
    per_device = solution.shape[0]
    seg_rows = per_device // levels_count
    block_size = block_values.shape[2]
    per_block = per_device // block_size
    row_index = lax.axis_index("row")
    col_index = lax.axis_index("col")
    gathered = row_gather(solution.astype(jnp.bfloat16))
    owner = block_columns // (per_block * col_count) ^ row_index
    local_block = owner * per_block + block_columns % per_block
    solution_blocks = gathered.reshape(row_count * per_block, block_size, -1)
    applied = block_product(block_values, solution_blocks, local_block, per_block)
    applied = applied.reshape(col_count, per_device, -1)
    residual = right_side - column_reduce(applied)
    device_index = row_index * col_count + col_index
    local_order = row_order - device_index * per_device
    permuted = residual[local_order]
    stacked = permuted.reshape(levels_count, seg_rows, -1)
    width = solution.shape[1]
    sep_bottom = 2 * col_count * seg_rows
    half_row = jax.ShapeDtypeStruct((seg_rows, width), jnp.bfloat16)
    full_row = jax.ShapeDtypeStruct((seg_rows, width), jnp.float32)
    spans = [sep_bottom * 2**k for k in range(levels_count)]
    offsets = [sep_bottom * (2**k - 1) for k in range(levels_count)]
    owns = [device_index % (2 ** (k + 1) * col_count) for k in range(levels_count)]
    lowered = []
    places = []
    for depth_k in range(levels_count - 1):
        front = row_index // 2 ** (depth_k + 1)
        chosen = lax.dynamic_slice_in_dim(
            update_rows[depth_k], front * spans[depth_k], spans[depth_k]
        )
        source = chosen // seg_rows ^ owns[depth_k + 1]
        places.append(source * seg_rows + chosen % seg_rows)
    incoming = None
    for depth_k in range(levels_count):
        current = stacked[depth_k]
        if depth_k > 0:
            current = current - incoming
        pieces = gather_pieces(current.astype(jnp.bfloat16), depth_k + 1)
        lower_rows = triangle_apply(
            lambda masks, *refs: lower_kernel(masks, offsets[depth_k], *refs),
            tri_inverses,
            owns[depth_k],
            pieces,
            half_row,
        )
        lowered.append(lower_rows)
        if depth_k + 1 < levels_count:
            begin, end = offsets[depth_k], offsets[depth_k] + spans[depth_k]
            kept, sent = scatter_update(
                lower_updates[begin:end], lower_rows, places[depth_k], depth_k + 2
            )
            incoming = front_reduce(kept, sent, depth_k + 2, seg_rows)
    corrections = []
    parent_rows = None
    for depth_k in reversed(range(levels_count)):
        rounded = lowered[depth_k]
        if depth_k + 1 < levels_count:
            begin, end = offsets[depth_k], offsets[depth_k] + spans[depth_k]
            rounded = pick_update(
                upper_updates[:, begin:end],
                gather_pieces(parent_rows, depth_k + 2),
                places[depth_k],
                rounded,
            )
        pieces = gather_pieces(rounded, depth_k + 1)
        if depth_k > 0:
            exact, parent_rows = triangle_apply(
                lambda masks, *refs: upper_kernel(masks, offsets[depth_k], *refs),
                tri_inverses,
                owns[depth_k],
                pieces,
                (full_row, half_row),
            )
            corrections.insert(0, exact)
    refined = triangle_apply(
        lambda masks, *refs: last_kernel(masks, offsets[0], levels_count, *refs),
        tri_inverses,
        owns[0],
        pieces,
        jax.ShapeDtypeStruct(solution.shape, jnp.float32),
        [solution] + corrections,
    )
    return (refined, residual)


def solution(mesh):
    in_specs = (
        P(BOTH, None),
        P(BOTH, None),
        P("row", "col", None, None),
        P("row", "col"),
        P(BOTH),
        P(BOTH, None),
        P(None, BOTH),
        P(BOTH, None),
        P(),
    )
    out_specs = (P(BOTH, None), P(BOTH, None))
    return jax.shard_map(
        on_device, mesh=mesh, in_specs=in_specs, out_specs=out_specs, check_vma=False
    )
```
